512 devices in a mesh: dp: 64 (over z, x, core), group: 8 (over y).
Axes of the slice: x: 4, y: 8, z: 8, core: 2. Of those that a mesh axis runs over, the one named last changes fastest.
Arguments:
- embeddings: bfloat16 [32768, 1024], P(('dp', 'group')), may hold values from -6 to 6
- cluster_ids: int32 [32768, 1], P(('dp', 'group')), may hold values from 0 to 63; in each aligned block of 64 rows (0 to 63, 64 to 127, ...) at most 2 rows name the same one
Outputs:
- density: float32 [32768], P(('dp', 'group'))
The draws below stay inside these ranges and needn't reach their ends.
Inputs may be any that keep to these rules, and one draw needn't show every extreme that they name: `cluster_ids`: among the 64 documents of one device no cluster appears more than 2 times, and some cluster appears exactly 2 times; every cluster appears somewhere.
All inputs are finite; a program needn't handle non-finite values.
Results may differ from the reference program's by a relative error of at most 0.0031.
Values may be sent and summed in bfloat16 or wider, within the bound.
A program may use at most 64 MiB of HBM per device.

```python
import math
import jax
import jax.numpy as jnp
import numpy as np
from jax import lax

E = 1024
DOC_DEV = 64
MOST = 2
CLUSTERS = 64
DOCS = 32768
CLUSTER_SLOTS = 1024
CLUSTER_MEAN = 512


def steps_of(key, dims, shards, low, high):
    gain, own = 1.0, jax.random.fold_in(key, 6)
    for dim, shards_of in shards:
        heights = jnp.exp(jax.random.uniform(jax.random.fold_in(own, dim), (shards_of,), jnp.float32, low / len(shards), high / len(shards)))
        gain = gain * jnp.repeat(heights, dims[dim] // shards_of).reshape([-1 if axis == dim else 1 for axis in range(len(dims))])
    return gain


def deal_out(own_key, own, number, rows, amount, top, reach, slope):
    order = jax.random.permutation(own_key, amount)
    packed, common = portions_of(amount, rows * top, reach, slope, True), portions_of(amount, rows * top, reach, slope, False)
    places = jnp.arange(amount)

    def named(sizes, turn):
        used = int((sizes > 0).sum())
        fixed = max(1, used // 4)
        moved = fixed + (places - fixed + turn * (used - fixed)) % max(1, amount - fixed)
        return jnp.zeros((amount,), jnp.int32).at[order[jnp.where(places < fixed, places, moved)]].set(jnp.asarray(sizes, jnp.int32))

    sizes = jnp.where(number % 4 == 0, named(packed, number // 4), named(common, number - number // 4 - 1))
    mixed = jax.random.permutation(jax.random.fold_in(own, 3), amount)
    giver, taker = mixed[0:amount // 2 * 2:2], mixed[1:amount // 2 * 2:2]
    margin = jnp.minimum(sizes[giver] - 1, reach - sizes[taker]) // 2
    margin = jnp.where((giver == order[0]) | (taker == order[0]) | (sizes[taker] == 0), 0, jnp.maximum(margin, 0))
    moved = jax.random.randint(jax.random.fold_in(own, 4), (amount // 2,), 0, 1 << 20) % (margin + 1)
    sizes = sizes.at[giver].add(-moved).at[taker].add(moved)
    items = jnp.searchsorted(jnp.cumsum(sizes), jnp.arange(rows * top), side="right").astype(jnp.int32)
    grid = items.reshape(top, rows).T
    grid = grid[jax.random.permutation(jax.random.fold_in(own, 1), rows)]
    turn = jax.random.randint(jax.random.fold_in(own, 2), (rows, 1), 0, top)
    return jnp.take_along_axis(grid, (jnp.arange(top)[None, :] + turn) % top, axis=1)


def portions_of(amount, total, reach, slope, full):
    loads = [(1 << 20) // math.isqrt(standing ** slope) + 1 for standing in range(1, amount + 1)]
    largest = reach if full else min(reach, max(-(-total // amount), total * loads[0] // sum(loads)))
    least = 1 if total - largest >= amount - 1 else 0
    counts, spare = [largest] + [least] * (amount - 1), total - largest - least * (amount - 1)
    while spare > 0:
        movable = [i for i in range(1, amount) if counts[i] < largest] or [i for i in range(1, amount) if counts[i] < reach]
        mass, budget = sum([loads[i] for i in movable]), spare
        for i in movable:
            addition = min(reach - counts[i], max(1, budget * loads[i] // mass), spare)
            counts[i] = counts[i] + addition
            spare = spare - addition
    return np.array(counts)


def scatter_about(rng, dims, scale, bound, cuts=(), kind=jnp.bfloat16):
    drawn = scale * jax.random.normal(rng, dims, jnp.float32)
    if cuts:
        drawn = drawn * steps_of(rng, dims, cuts, -0.22, 0.18)
    return jnp.clip(drawn, -bound, bound).astype(kind)


def setup_inputs(seed: int = 0) -> dict:
    arg_keys = jax.random.split(jax.random.key(seed), 3)
    embeddings = scatter_about(arg_keys[0], (DOCS, E), 1.0, 6.0, ((0, 512),))
    cluster_ids_keys = jax.random.split(jax.random.fold_in(arg_keys[1], 1), DOCS // DOC_DEV)
    cluster_ids_turns = jax.random.permutation(jax.random.fold_in(arg_keys[1], 3), DOCS // DOC_DEV)
    cluster_ids = jax.vmap(lambda own, number: deal_out(jax.random.fold_in(arg_keys[1], 2), own, number, DOC_DEV, CLUSTERS, 1, MOST, 1))(cluster_ids_keys, cluster_ids_turns).reshape((DOCS, 1))
    return {"embeddings": embeddings, "cluster_ids": cluster_ids}


epsilon = 1e-06

def reference(embeddings, cluster_ids):
    widened = embeddings.astype(jnp.float32)
    normed = (widened / jnp.sqrt(lax.optimization_barrier(jnp.sum(widened * widened, axis=1, keepdims=True)) + epsilon)).astype(jnp.bfloat16)
    cluster = cluster_ids[:, 0].astype(jnp.int32)
    sorted_pos = jnp.argsort(cluster, stable=True).astype(jnp.int32)
    labels = jnp.arange(CLUSTERS, dtype=jnp.int32)
    cluster_sizes = lax.optimization_barrier(jnp.sum((cluster[None, :] == labels[:, None]).astype(jnp.int32), axis=1))
    first_pos = (jnp.cumsum(cluster_sizes) - cluster_sizes).astype(jnp.int32)
    sharpen = math.sqrt(E)

    def cluster_terms(which):
        position = jnp.arange(CLUSTER_SLOTS, dtype=jnp.int32)
        present = position < cluster_sizes[which]
        members = sorted_pos[jnp.minimum(first_pos[which] + position, DOCS - 1).astype(jnp.int32)]
        member_rows = normed[members].astype(jnp.float32)
        scores = jnp.dot(member_rows, member_rows.T, precision=lax.Precision.HIGHEST)
        distinct = present[:, None] & present[None, :] & (position[:, None] != position[None, :])
        weights = jnp.where(distinct, jnp.exp(scores * sharpen), jnp.float32(0.0))
        row_sums = lax.optimization_barrier(jnp.sum(weights, axis=1))
        return (members, jnp.where(present, row_sums, jnp.float32(0.0)))
    members_all, sums_all = lax.map(cluster_terms, labels)
    totals = jnp.zeros((DOCS,), jnp.float32).at[members_all.reshape(-1)].add(sums_all.reshape(-1))
    return totals / CLUSTER_MEAN
```

```python
import functools
import math

import jax
import jax.numpy as jnp
from jax import lax
from jax.experimental import pallas as pl
from jax.experimental.pallas import tpu as pltpu
from jax.sharding import PartitionSpec as P

MESH = pl.DeviceIdType.MESH
epsilon = 1e-06
Z, X, Y, CORES = 8, 4, 8, 2
SLOTS = Z * Y
PER = 2
ROWS = SLOTS * PER
CHUNKS = 8
LANES = 128
OFFSETS = [(dz, dy) for dz in range(Z) for dy in range(Y)]
GROUP_ORDER = [4, 3, 5, 2, 6, 1, 7, 0]
ROW_ORDER = [4, 3, 5, 2, 6, 1, 7, 0]


def wrap(value, size):
    return lax.rem(value + size, size)


def eye(size):
    return lax.broadcasted_iota(jnp.int32, (size, size), 0) == lax.broadcasted_iota(
        jnp.int32, (size, size), 1
    )


def permutation(tile_major):
    out = lax.broadcasted_iota(jnp.int32, (ROWS, ROWS), 0)
    src = lax.broadcasted_iota(jnp.int32, (ROWS, ROWS), 1)
    wanted = (lax.rem(lax.div(out, 2), 8) * 8 + lax.div(out, 16)) * 2 + lax.rem(out, 2)
    return (src == wanted).astype(jnp.float32).astype(jnp.bfloat16)


def dot_t(left, right):
    return lax.dot_general(
        left, right, (((1,), (1,)), ((), ())), preferred_element_type=jnp.float32
    )


def kernel(
    sharpen,
    x_ref,
    ids_ref,
    out_ref,
    send_buf,
    raw,
    blocks,
    part_send,
    part_recv,
    ret_src,
    ret,
    a2a_send,
    a2a_recv,
    fwd_send,
    fwd_recv,
    part_ssem,
    part_rsem,
    ret_ssem,
    ret_rsem,
):
    dp, y = lax.axis_index("dp"), lax.axis_index("group")
    z = lax.div(dp, X * CORES)
    x = lax.rem(lax.div(dp, CORES), X)
    core = lax.rem(dp, CORES)
    other = 1 - core
    right, left = wrap(x + 1, X), wrap(x - 1, X)

    def device(zz, xx, cc, yy):
        return ((zz * X + xx) * CORES + cc, yy)

    def plane(dz, dy):
        return device(wrap(z + dz, Z), x, core, wrap(y + dy, Y))

    partner = device(z, x, other, y)
    swap = lax.div(right, 2)
    own_swap = lax.div(x, 2)
    to_right = device(z, right, core + swap * (1 - 2 * core), y)
    to_left = device(z, left, core, y)
    from_right = device(z, right, core, y)
    from_left = device(z, left, core + own_swap * (1 - 2 * core), y)

    barrier = pltpu.get_barrier_semaphore()
    for dz, dy in OFFSETS[1:]:
        pl.semaphore_signal(barrier, inc=1, device_id=plane(dz, dy), device_id_type=MESH)
    near = [partner] + [device(z, xx, cc, y) for xx in (left, right) for cc in (0, 1)]
    for target in near:
        pl.semaphore_signal(barrier, inc=1, device_id=target, device_id_type=MESH)

    docs = x_ref.shape[0]
    widened = x_ref[...].astype(jnp.float32)
    normed = (
        widened / jnp.sqrt(jnp.sum(widened * widened, axis=1, keepdims=True) + epsilon)
    ).astype(jnp.bfloat16)

    ids_row = ids_ref[...]
    ids_col = jnp.sum(jnp.where(eye(docs), ids_row, 0), axis=1, keepdims=True)
    earlier = lax.broadcasted_iota(jnp.int32, (docs, docs), 0) < lax.broadcasted_iota(
        jnp.int32, (docs, docs), 1
    )
    within = jnp.sum(jnp.where((ids_col == ids_row) & earlier, 1, 0), axis=0, keepdims=True)
    slot_row = lax.broadcasted_iota(jnp.int32, (ROWS, 1), 0)
    owner = (
        lax.rem(z + lax.div(slot_row, 2 * Y), Z) * Y
        + lax.rem(y + lax.rem(lax.div(slot_row, 2), Y), Y)
    )
    chosen = (owner == ids_row) & (lax.rem(slot_row, 2) == within)
    onehot = jnp.where(chosen, 1.0, 0.0)
    empty = jnp.sum(onehot, axis=1, keepdims=True) == 0.0

    packed = jnp.dot(onehot.astype(jnp.bfloat16), normed, preferred_element_type=jnp.float32)
    first = lax.broadcasted_iota(jnp.int32, packed.shape, 1) == 0
    packed = jnp.where(empty & first, 2.0, packed).astype(jnp.bfloat16)
    perm = permutation(True)
    stacked = jnp.concatenate(
        [
            jnp.concatenate(
                [packed[16 * g : 16 * g + 16, LANES * k : LANES * k + LANES] for k in range(CHUNKS)],
                axis=0,
            )
            for g in range(Z)
        ],
        axis=1,
    )
    tiles = jnp.dot(perm, stacked, preferred_element_type=jnp.float32).astype(jnp.bfloat16)
    for g in range(Z):
        for dy in range(Y):
            tile = tiles[16 * dy : 16 * dy + 16, LANES * g : LANES * g + LANES]
            if g == 0 and dy == 0:
                raw[0, 0] = tile
            else:
                send_buf[g * Y + dy] = tile

    pl.semaphore_wait(barrier, SLOTS - 1 + len(near))

    for dz in GROUP_ORDER:
        for dy in ROW_ORDER:
            if (dz, dy) == (0, 0):
                continue
            slot = dz * Y + dy
            pltpu.make_async_remote_copy(
                src_ref=send_buf.at[slot],
                dst_ref=raw.at[0, slot],
                send_sem=a2a_send,
                recv_sem=a2a_recv.at[dz],
                device_id=plane(dz, dy),
                device_id_type=MESH,
            ).start()

    def convert(which, row, g):
        got = raw[which, g * Y : (g + 1) * Y].reshape(ROWS, LANES)
        turned = jnp.dot(perm, got, preferred_element_type=jnp.float32).astype(jnp.bfloat16)
        for k in range(CHUNKS):
            blocks[row + 16 * g : row + 16 * g + 16, LANES * k : LANES * k + LANES] = turned[
                16 * k : 16 * k + 16
            ]

    starts = (ROWS, 2 * ROWS, 0, 3 * ROWS)
    targets = (None, partner, to_left, to_right)

    def forward(which, g):
        return pltpu.make_async_remote_copy(
            src_ref=raw.at[0, pl.ds(g * Y, Y)],
            dst_ref=raw.at[which, pl.ds(g * Y, Y)],
            send_sem=fwd_send.at[which - 1, g],
            recv_sem=fwd_recv.at[which - 1, g],
            device_id=targets[which],
            device_id_type=MESH,
        )

    for g in GROUP_ORDER:
        skip = 1 if g == 0 else 0
        arrived = raw.at[0, pl.ds(g * Y + skip, Y - skip)]
        pltpu.make_async_copy(arrived, arrived, a2a_recv.at[g]).wait()
        for which in (3, 2, 1):
            forward(which, g).start()
        convert(0, starts[0], g)
    for g in GROUP_ORDER:
        for which in (1, 2, 3):
            forward(which, g).wait_recv()
            convert(which, starts[which], g)

    from_r, own, mate, from_l = (pl.ds(start, ROWS) for start in (0, ROWS, 2 * ROWS, 3 * ROWS))

    def column_sums(rows, columns, diagonal_at=None):
        source = blocks[rows, :]
        scores = dot_t(source, blocks[columns, :])
        keep = source[:, 0:1].astype(jnp.float32) < 1.5
        if diagonal_at is not None:
            keep = keep & (
                lax.broadcasted_iota(jnp.int32, scores.shape, 0)
                != lax.broadcasted_iota(jnp.int32, scores.shape, 1) + diagonal_at
            )
        return jnp.sum(
            jnp.where(keep, jnp.exp(scores * sharpen), 0.0), axis=0, keepdims=True
        )

    part_send[0] = column_sums(pl.ds(ROWS, 3 * ROWS), from_r)
    both = column_sums(from_r, pl.ds(2 * ROWS, 2 * ROWS))
    part_send[1] = both[:, :ROWS]
    part_send[2] = both[:, ROWS:]

    def part(which):
        return pltpu.make_async_remote_copy(
            src_ref=part_send.at[which],
            dst_ref=part_recv.at[which],
            send_sem=part_ssem.at[which],
            recv_sem=part_rsem.at[which],
            device_id=(from_right, partner, from_left)[which],
            device_id_type=MESH,
        )

    for which in range(3):
        part(which).start()
    total = column_sums(pl.ds(0, 3 * ROWS), own, diagonal_at=ROWS)
    for which in range(3):
        part(which).wait_recv()
        total = total + part_recv[which]
    total = total * (1.0 / (docs * Y))
    ret_src[0] = total
    ret[0] = total
    for dz in GROUP_ORDER:
        for dy in ROW_ORDER:
            if (dz, dy) == (0, 0):
                continue
            pltpu.make_async_remote_copy(
                src_ref=ret_src.at[0],
                dst_ref=ret.at[dz * Y + dy],
                send_sem=ret_ssem,
                recv_sem=ret_rsem,
                device_id=plane(-dz, -dy),
                device_id_type=MESH,
            ).start()

    sent = send_buf.at[pl.ds(1, SLOTS - 1)]
    pltpu.make_async_copy(sent, sent, a2a_send).wait()
    for g in range(Z):
        for which in (1, 2, 3):
            forward(which, g).wait_send()
    for which in range(3):
        part(which).wait_send()
    back = ret.at[pl.ds(1, SLOTS - 1)]
    pltpu.make_async_copy(back, back, ret_rsem).wait()

    lane = lax.broadcasted_iota(jnp.int32, (SLOTS, 1, LANES), 2)
    slot = lax.broadcasted_iota(jnp.int32, (SLOTS, 1, LANES), 0)
    mine = jnp.sum(jnp.where(lax.div(lane, 2) == slot, ret[...], 0.0), axis=0)
    column = jnp.sum(jnp.where(eye(ROWS), mine, 0.0), axis=1, keepdims=True)
    out_ref[...] = jnp.sum(jnp.where(chosen, column, 0.0), axis=0, keepdims=True)
    pltpu.make_async_copy(back, back, ret_ssem).wait()


def shards(embeddings, cluster_ids):
    docs, width = embeddings.shape
    vmem = pl.BlockSpec(memory_space=pltpu.VMEM)
    bf16, f32 = jnp.bfloat16, jnp.float32
    out = pl.pallas_call(
        functools.partial(kernel, math.sqrt(width)),
        out_shape=jax.ShapeDtypeStruct((1, docs), f32),
        in_specs=[vmem, vmem],
        out_specs=vmem,
        scratch_shapes=[
            pltpu.VMEM((SLOTS, 16, LANES), bf16),
            pltpu.VMEM((4, SLOTS, 16, LANES), bf16),
            pltpu.VMEM((4 * ROWS, width), bf16),
            pltpu.VMEM((3, 1, LANES), f32),
            pltpu.VMEM((3, 1, LANES), f32),
            pltpu.VMEM((1, 1, LANES), f32),
            pltpu.VMEM((SLOTS, 1, LANES), f32),
            pltpu.SemaphoreType.DMA,
            pltpu.SemaphoreType.DMA((Z,)),
            pltpu.SemaphoreType.DMA((3, Z)),
            pltpu.SemaphoreType.DMA((3, Z)),
            pltpu.SemaphoreType.DMA((3,)),
            pltpu.SemaphoreType.DMA((3,)),
            pltpu.SemaphoreType.DMA,
            pltpu.SemaphoreType.DMA,
        ],
        compiler_params=pltpu.CompilerParams(collective_id=0, has_side_effects=True),
    )(embeddings, cluster_ids.reshape(1, docs))
    return out.reshape(docs)


def solution(mesh):
    placed = (P(("dp", "group"), None), P(("dp", "group"), None))
    return jax.shard_map(
        shards, mesh=mesh, in_specs=placed, out_specs=P(("dp", "group")), check_vma=False
    )
```

```python
import functools
import math

import jax
import jax.numpy as jnp
from jax import lax
from jax.experimental import pallas as pl
from jax.experimental.pallas import tpu as pltpu
from jax.sharding import PartitionSpec as P

MESH = pl.DeviceIdType.MESH
epsilon = 1e-06
Z, X, Y, CORES = 8, 4, 8, 2
SLOTS = Z * Y
PER = 2
ROWS = SLOTS * PER
CHUNKS = 8
LANES = 128


def hops(offset):
    dz, dy = offset
    return min(dz, Z - dz) + min(dy, Y - dy)


OFFSETS = sorted([(dz, dy) for dz in range(Z) for dy in range(Y)], key=lambda at: (hops(at), at))
GROUPS = SLOTS // 8


def wrap(value, size):
    return lax.rem(value + size, size)


def eye(size):
    return lax.broadcasted_iota(jnp.int32, (size, size), 0) == lax.broadcasted_iota(
        jnp.int32, (size, size), 1
    )


def permutation(tile_major):
    out = lax.broadcasted_iota(jnp.int32, (ROWS, ROWS), 0)
    src = lax.broadcasted_iota(jnp.int32, (ROWS, ROWS), 1)
    wanted = (lax.rem(lax.div(out, 2), 8) * 8 + lax.div(out, 16)) * 2 + lax.rem(out, 2)
    return (src == wanted).astype(jnp.float32).astype(jnp.bfloat16)


def dot_t(left, right):
    return lax.dot_general(
        left, right, (((1,), (1,)), ((), ())), preferred_element_type=jnp.float32
    )


def kernel(
    sharpen,
    x_hbm,
    ids_hbm,
    out_ref,
    send_buf,
    raw,
    blocks,
    part_send,
    part_recv,
    ret_src,
    ret,
    a2a_send,
    a2a_recv,
    fwd_send,
    fwd_recv,
    part_ssem,
    part_rsem,
    ret_ssem,
    ret_rsem,
    x_ref,
    ids_ref,
    in_sem,
):
    dp, y = lax.axis_index("dp"), lax.axis_index("group")
    z = lax.div(dp, X * CORES)
    x = lax.rem(lax.div(dp, CORES), X)
    core = lax.rem(dp, CORES)
    other = 1 - core
    right, left = wrap(x + 1, X), wrap(x - 1, X)

    def device(zz, xx, cc, yy):
        return ((zz * X + xx) * CORES + cc, yy)

    def plane(dz, dy):
        return device(wrap(z + dz, Z), x, core, wrap(y + dy, Y))

    partner = device(z, x, other, y)
    swap = lax.div(right, 2)
    own_swap = lax.div(x, 2)
    to_right = device(z, right, core + swap * (1 - 2 * core), y)
    to_left = device(z, left, core, y)
    from_right = device(z, right, core, y)
    from_left = device(z, left, core + own_swap * (1 - 2 * core), y)

    load_x = pltpu.make_async_copy(x_hbm, x_ref, in_sem.at[0])
    load_ids = pltpu.make_async_copy(ids_hbm, ids_ref, in_sem.at[1])
    load_x.start()
    load_ids.start()
    barrier = pltpu.get_barrier_semaphore()
    for dz, dy in OFFSETS[:0:-1]:
        pl.semaphore_signal(barrier, inc=1, device_id=plane(dz, dy), device_id_type=MESH)
    near = [partner] + [device(z, xx, cc, y) for xx in (left, right) for cc in (0, 1)]
    for target in near:
        pl.semaphore_signal(barrier, inc=1, device_id=target, device_id_type=MESH)

    load_x.wait()
    load_ids.wait()

    docs = x_ref.shape[0]
    widened = x_ref[...].astype(jnp.float32)
    normed = (
        widened / jnp.sqrt(jnp.sum(widened * widened, axis=1, keepdims=True) + epsilon)
    ).astype(jnp.bfloat16)

    ids_row = ids_ref[...]
    ids_col = jnp.sum(jnp.where(eye(docs), ids_row, 0), axis=1, keepdims=True)
    earlier = lax.broadcasted_iota(jnp.int32, (docs, docs), 0) < lax.broadcasted_iota(
        jnp.int32, (docs, docs), 1
    )
    within = jnp.sum(jnp.where((ids_col == ids_row) & earlier, 1, 0), axis=0, keepdims=True)
    slot_row = lax.broadcasted_iota(jnp.int32, (ROWS, 1), 0)
    slot = lax.div(slot_row, 2)
    owner_z, owner_y = z + jnp.zeros_like(slot), y + jnp.zeros_like(slot)
    for k, (dz, dy) in enumerate(OFFSETS):
        owner_z = owner_z + jnp.where(slot == k, dz, 0)
        owner_y = owner_y + jnp.where(slot == k, dy, 0)
    owner = lax.rem(owner_z, Z) * Y + lax.rem(owner_y, Y)
    chosen = (owner == ids_row) & (lax.rem(slot_row, 2) == within)
    onehot = jnp.where(chosen, 1.0, 0.0)
    empty = jnp.sum(onehot, axis=1, keepdims=True) == 0.0

    packed = jnp.dot(onehot.astype(jnp.bfloat16), normed, preferred_element_type=jnp.float32)
    first = lax.broadcasted_iota(jnp.int32, packed.shape, 1) == 0
    packed = jnp.where(empty & first, 2.0, packed).astype(jnp.bfloat16)
    perm = permutation(True)
    stacked = jnp.concatenate(
        [
            jnp.concatenate(
                [packed[16 * g : 16 * g + 16, LANES * k : LANES * k + LANES] for k in range(CHUNKS)],
                axis=0,
            )
            for g in range(GROUPS)
        ],
        axis=1,
    )
    tiles = jnp.dot(perm, stacked, preferred_element_type=jnp.float32).astype(jnp.bfloat16)
    for k in range(SLOTS):
        g, row = k // 8, 16 * (k % 8)
        tile = tiles[row : row + 16, LANES * g : LANES * g + LANES]
        if k == 0:
            raw[0, 0] = tile
        else:
            send_buf[k] = tile

    pl.semaphore_wait(barrier, SLOTS - 1 + len(near))

    for k, (dz, dy) in list(enumerate(OFFSETS))[1:]:
        pltpu.make_async_remote_copy(
            src_ref=send_buf.at[k],
            dst_ref=raw.at[0, k],
            send_sem=a2a_send,
            recv_sem=a2a_recv.at[k // 8],
            device_id=plane(dz, dy),
            device_id_type=MESH,
        ).start()

    def convert(which, row, g):
        got = raw[which, 8 * g : 8 * g + 8].reshape(ROWS, LANES)
        turned = jnp.dot(perm, got, preferred_element_type=jnp.float32).astype(jnp.bfloat16)
        for k in range(CHUNKS):
            blocks[row + 16 * g : row + 16 * g + 16, LANES * k : LANES * k + LANES] = turned[
                16 * k : 16 * k + 16
            ]

    starts = (ROWS, 2 * ROWS, 0, 3 * ROWS)
    targets = (None, partner, to_left, to_right)

    def forward(which, g):
        return pltpu.make_async_remote_copy(
            src_ref=raw.at[0, pl.ds(8 * g, 8)],
            dst_ref=raw.at[which, pl.ds(8 * g, 8)],
            send_sem=fwd_send.at[which - 1, g],
            recv_sem=fwd_recv.at[which - 1, g],
            device_id=targets[which],
            device_id_type=MESH,
        )

    for g in range(GROUPS):
        skip = 1 if g == 0 else 0
        arrived = raw.at[0, pl.ds(8 * g + skip, 8 - skip)]
        pltpu.make_async_copy(arrived, arrived, a2a_recv.at[g]).wait()
        for which in (3, 2, 1):
            forward(which, g).start()
        convert(0, starts[0], g)
    for g in range(GROUPS):
        for which in (1, 2, 3):
            forward(which, g).wait_recv()
            convert(which, starts[which], g)

    from_r, own, mate, from_l = (pl.ds(start, ROWS) for start in (0, ROWS, 2 * ROWS, 3 * ROWS))

    def column_sums(rows, columns, diagonal_at=None):
        source = blocks[rows, :]
        scores = dot_t(source, blocks[columns, :])
        keep = source[:, 0:1].astype(jnp.float32) < 1.5
        if diagonal_at is not None:
            keep = keep & (
                lax.broadcasted_iota(jnp.int32, scores.shape, 0)
                != lax.broadcasted_iota(jnp.int32, scores.shape, 1) + diagonal_at
            )
        return jnp.sum(
            jnp.where(keep, jnp.exp(scores * sharpen), 0.0), axis=0, keepdims=True
        )

    part_send[0] = column_sums(pl.ds(ROWS, 3 * ROWS), from_r)
    both = column_sums(from_r, pl.ds(2 * ROWS, 2 * ROWS))
    part_send[1] = both[:, :ROWS]
    part_send[2] = both[:, ROWS:]

    def part(which):
        return pltpu.make_async_remote_copy(
            src_ref=part_send.at[which],
            dst_ref=part_recv.at[which],
            send_sem=part_ssem.at[which],
            recv_sem=part_rsem.at[which],
            device_id=(from_right, partner, from_left)[which],
            device_id_type=MESH,
        )

    for which in range(3):
        part(which).start()
    total = column_sums(pl.ds(0, 3 * ROWS), own, diagonal_at=ROWS)
    for which in range(3):
        part(which).wait_recv()
        total = total + part_recv[which]
    ret_src[0] = total
    ret[0] = total
    for k, (dz, dy) in list(enumerate(OFFSETS))[:0:-1]:
        pltpu.make_async_remote_copy(
            src_ref=ret_src.at[0],
            dst_ref=ret.at[k],
            send_sem=ret_ssem,
            recv_sem=ret_rsem,
            device_id=plane(-dz, -dy),
            device_id_type=MESH,
        ).start()

    sent = send_buf.at[pl.ds(1, SLOTS - 1)]
    pltpu.make_async_copy(sent, sent, a2a_send).wait()
    for g in range(GROUPS):
        for which in (1, 2, 3):
            forward(which, g).wait_send()
    for which in range(3):
        part(which).wait_send()
    back = ret.at[pl.ds(1, SLOTS - 1)]
    pltpu.make_async_copy(back, back, ret_rsem).wait()

    lane = lax.broadcasted_iota(jnp.int32, (SLOTS, 1, LANES), 2)
    at = lax.broadcasted_iota(jnp.int32, (SLOTS, 1, LANES), 0)
    mine = jnp.sum(jnp.where(lax.div(lane, 2) == at, ret[...], 0.0), axis=0)
    column = jnp.sum(jnp.where(eye(ROWS), mine, 0.0), axis=1, keepdims=True)
    out_ref[...] = jnp.sum(jnp.where(chosen, column, 0.0), axis=0, keepdims=True)
    pltpu.make_async_copy(back, back, ret_ssem).wait()


def shards(embeddings, cluster_ids):
    docs, width = embeddings.shape
    vmem = pl.BlockSpec(memory_space=pltpu.VMEM)
    bf16, f32 = jnp.bfloat16, jnp.float32
    out = pl.pallas_call(
        functools.partial(kernel, math.sqrt(width)),
        out_shape=jax.ShapeDtypeStruct((1, docs), f32),
        in_specs=[pl.BlockSpec(memory_space=pl.ANY)] * 2,
        out_specs=vmem,
        scratch_shapes=[
            pltpu.VMEM((SLOTS, 16, LANES), bf16),
            pltpu.VMEM((4, SLOTS, 16, LANES), bf16),
            pltpu.VMEM((4 * ROWS, width), bf16),
            pltpu.VMEM((3, 1, LANES), f32),
            pltpu.VMEM((3, 1, LANES), f32),
            pltpu.VMEM((1, 1, LANES), f32),
            pltpu.VMEM((SLOTS, 1, LANES), f32),
            pltpu.SemaphoreType.DMA,
            pltpu.SemaphoreType.DMA((GROUPS,)),
            pltpu.SemaphoreType.DMA((3, GROUPS)),
            pltpu.SemaphoreType.DMA((3, GROUPS)),
            pltpu.SemaphoreType.DMA((3,)),
            pltpu.SemaphoreType.DMA((3,)),
            pltpu.SemaphoreType.DMA,
            pltpu.SemaphoreType.DMA,
            pltpu.VMEM((docs, width), bf16),
            pltpu.VMEM((1, docs), jnp.int32),
            pltpu.SemaphoreType.DMA((2,)),
        ],
        compiler_params=pltpu.CompilerParams(collective_id=0, has_side_effects=True),
    )(embeddings, cluster_ids.reshape(1, docs))
    return out.reshape(docs) * (1.0 / (docs * Y))


def solution(mesh):
    placed = (P(("dp", "group"), None), P(("dp", "group"), None))
    return jax.shard_map(
        shards, mesh=mesh, in_specs=placed, out_specs=P(("dp", "group")), check_vma=False
    )
```

```python
import functools
import math

import jax
import jax.numpy as jnp
from jax import lax
from jax.experimental import pallas as pl
from jax.experimental.pallas import tpu as pltpu
from jax.sharding import PartitionSpec as P

MESH = pl.DeviceIdType.MESH
epsilon = 1e-06
Z, X, Y, CORES = 8, 4, 8, 2
SLOTS = Z * Y
PER = 2
ROWS = SLOTS * PER
CHUNKS = 8
LANES = 128

RING = 8
NEAREST = [0, 1, 7, 2, 6, 3, 5, 4]
PIECES = [(0, 1), (1, 8)]
GROUPS = SLOTS // RING
FIRST_ORDER = [7, 6, 5, 4, 3, 2, 1]
SECOND_ORDER = [1, 2, 3, 4, 5, 6, 7]


def offset_of(place):
    half = lax.div(place + 1, 2)
    return jnp.where(lax.rem(place, 2) == 1, half, lax.rem(RING - half, RING))


def wrap(value, size):
    return lax.rem(value + size, size)


def eye(size):
    return lax.broadcasted_iota(jnp.int32, (size, size), 0) == lax.broadcasted_iota(
        jnp.int32, (size, size), 1
    )


def permutation(tile_major):
    out = lax.broadcasted_iota(jnp.int32, (ROWS, ROWS), 0)
    src = lax.broadcasted_iota(jnp.int32, (ROWS, ROWS), 1)
    wanted = (lax.rem(lax.div(out, 2), 8) * 8 + lax.div(out, 16)) * 2 + lax.rem(out, 2)
    return (src == wanted).astype(jnp.float32).astype(jnp.bfloat16)


def dot_t(left, right):
    return lax.dot_general(
        left, right, (((1,), (1,)), ((), ())), preferred_element_type=jnp.float32
    )


def kernel(
    sharpen,
    x_hbm,
    ids_hbm,
    out_ref,
    send_buf,
    middle,
    raw,
    blocks,
    part_send,
    part_recv,
    ret_src,
    ret,
    one_send,
    one_recv,
    two_send,
    two_recv,
    fwd_send,
    fwd_recv,
    part_ssem,
    part_rsem,
    ret_ssem,
    ret_rsem,
    x_ref,
    ids_ref,
    in_sem,
):
    dp, y = lax.axis_index("dp"), lax.axis_index("group")
    z = lax.div(dp, X * CORES)
    x = lax.rem(lax.div(dp, CORES), X)
    core = lax.rem(dp, CORES)
    other = 1 - core
    right, left = wrap(x + 1, X), wrap(x - 1, X)

    def device(zz, xx, cc, yy):
        return ((zz * X + xx) * CORES + cc, yy)

    def plane(first, second):
        dz = second + core * (first - second)
        dy = first + core * (second - first)
        return device(wrap(z + dz, Z), x, core, wrap(y + dy, Y))

    partner = device(z, x, other, y)
    swap = lax.div(right, 2)
    own_swap = lax.div(x, 2)
    to_right = device(z, right, core + swap * (1 - 2 * core), y)
    to_left = device(z, left, core, y)
    from_right = device(z, right, core, y)
    from_left = device(z, left, core + own_swap * (1 - 2 * core), y)

    load_x = pltpu.make_async_copy(x_hbm, x_ref, in_sem.at[0])
    load_ids = pltpu.make_async_copy(ids_hbm, ids_ref, in_sem.at[1])
    load_x.start()
    load_ids.start()
    barrier = pltpu.get_barrier_semaphore()
    for away in NEAREST[:0:-1]:
        for target in (plane(away, 0), plane(0, away)):
            pl.semaphore_signal(barrier, inc=1, device_id=target, device_id_type=MESH)
    near = [partner] + [device(z, xx, cc, y) for xx in (left, right) for cc in (0, 1)]
    for target in near:
        pl.semaphore_signal(barrier, inc=1, device_id=target, device_id_type=MESH)

    load_x.wait()
    load_ids.wait()

    docs = x_ref.shape[0]
    widened = x_ref[...].astype(jnp.float32)
    normed = (
        widened / jnp.sqrt(jnp.sum(widened * widened, axis=1, keepdims=True) + epsilon)
    ).astype(jnp.bfloat16)

    ids_row = ids_ref[...]
    ids_col = jnp.sum(jnp.where(eye(docs), ids_row, 0), axis=1, keepdims=True)
    earlier = lax.broadcasted_iota(jnp.int32, (docs, docs), 0) < lax.broadcasted_iota(
        jnp.int32, (docs, docs), 1
    )
    within = jnp.sum(jnp.where((ids_col == ids_row) & earlier, 1, 0), axis=0, keepdims=True)
    slot_row = lax.broadcasted_iota(jnp.int32, (ROWS, 1), 0)
    slot = lax.div(slot_row, 2)
    first, second = offset_of(lax.rem(slot, RING)), offset_of(lax.div(slot, RING))
    owner_z = lax.rem(z + second + core * (first - second), Z)
    owner_y = lax.rem(y + first + core * (second - first), Y)
    owner = owner_z * Y + owner_y
    chosen = (owner == ids_row) & (lax.rem(slot_row, 2) == within)
    onehot = jnp.where(chosen, 1.0, 0.0)
    empty = jnp.sum(onehot, axis=1, keepdims=True) == 0.0

    packed = jnp.dot(onehot.astype(jnp.bfloat16), normed, preferred_element_type=jnp.float32)
    first = lax.broadcasted_iota(jnp.int32, packed.shape, 1) == 0
    packed = jnp.where(empty & first, 2.0, packed).astype(jnp.bfloat16)
    perm = permutation(True)
    stacked = jnp.concatenate(
        [
            jnp.concatenate(
                [packed[16 * g : 16 * g + 16, LANES * k : LANES * k + LANES] for k in range(CHUNKS)],
                axis=0,
            )
            for g in range(GROUPS)
        ],
        axis=1,
    )
    tiles = jnp.dot(perm, stacked, preferred_element_type=jnp.float32).astype(jnp.bfloat16)
    for k in range(SLOTS):
        g, row = k // 8, 16 * (k % 8)
        tile = tiles[row : row + 16, LANES * g : LANES * g + LANES]
        if k % RING == 0:
            middle[g, 0] = tile
        else:
            send_buf[k % RING, g] = tile

    pl.semaphore_wait(barrier, 2 * (RING - 1) + len(near))

    def along_first(a):
        return pltpu.make_async_remote_copy(
            src_ref=send_buf.at[a],
            dst_ref=middle.at[pl.ds(0, RING), a],
            send_sem=one_send,
            recv_sem=one_recv.at[a],
            device_id=plane(NEAREST[a], 0),
            device_id_type=MESH,
        )

    def along_second(b, piece):
        low, high = PIECES[piece]
        return pltpu.make_async_remote_copy(
            src_ref=middle.at[b, pl.ds(low, high - low)],
            dst_ref=raw.at[0, pl.ds(b * RING + low, high - low)],
            send_sem=two_send,
            recv_sem=two_recv.at[b, piece],
            device_id=plane(0, NEAREST[b]),
            device_id_type=MESH,
        )

    for a in FIRST_ORDER:
        along_first(a).start()
    for piece, (low, high) in enumerate(PIECES):
        for a in range(max(low, 1), high):
            along_first(a).wait_recv()
        for b in SECOND_ORDER:
            along_second(b, piece).start()

    def convert(which, row, g):
        got = middle[0] if which == 0 and g == 0 else raw[which, 8 * g : 8 * g + 8]
        got = got.reshape(ROWS, LANES)
        turned = jnp.dot(perm, got, preferred_element_type=jnp.float32).astype(jnp.bfloat16)
        for k in range(CHUNKS):
            blocks[row + 16 * g : row + 16 * g + 16, LANES * k : LANES * k + LANES] = turned[
                16 * k : 16 * k + 16
            ]

    starts = (ROWS, 2 * ROWS, 0, 3 * ROWS)
    targets = (None, partner, to_left, to_right)

    def forward(which, g):
        return pltpu.make_async_remote_copy(
            src_ref=middle.at[0] if g == 0 else raw.at[0, pl.ds(8 * g, 8)],
            dst_ref=raw.at[which, pl.ds(8 * g, 8)],
            send_sem=fwd_send.at[which - 1, g],
            recv_sem=fwd_recv.at[which - 1, g],
            device_id=targets[which],
            device_id_type=MESH,
        )

    for g in range(GROUPS):
        if g > 0:
            for piece in range(len(PIECES)):
                along_second(g, piece).wait_recv()
        for which in (3, 2, 1):
            forward(which, g).start()
        convert(0, starts[0], g)
    for g in range(GROUPS):
        for which in (1, 2, 3):
            forward(which, g).wait_recv()
            convert(which, starts[which], g)

    from_r, own, mate, from_l = (pl.ds(start, ROWS) for start in (0, ROWS, 2 * ROWS, 3 * ROWS))

    def column_sums(rows, columns, diagonal_at=None):
        source = blocks[rows, :]
        scores = dot_t(source, blocks[columns, :])
        keep = source[:, 0:1].astype(jnp.float32) < 1.5
        if diagonal_at is not None:
            keep = keep & (
                lax.broadcasted_iota(jnp.int32, scores.shape, 0)
                != lax.broadcasted_iota(jnp.int32, scores.shape, 1) + diagonal_at
            )
        return jnp.sum(
            jnp.where(keep, jnp.exp(scores * sharpen), 0.0), axis=0, keepdims=True
        )

    part_send[0] = column_sums(pl.ds(ROWS, 3 * ROWS), from_r)
    both = column_sums(from_r, pl.ds(2 * ROWS, 2 * ROWS))
    part_send[1] = both[:, :ROWS]
    part_send[2] = both[:, ROWS:]

    def part(which):
        return pltpu.make_async_remote_copy(
            src_ref=part_send.at[which],
            dst_ref=part_recv.at[which],
            send_sem=part_ssem.at[which],
            recv_sem=part_rsem.at[which],
            device_id=(from_right, partner, from_left)[which],
            device_id_type=MESH,
        )

    for which in range(3):
        part(which).start()
    total = column_sums(pl.ds(0, 3 * ROWS), own, diagonal_at=ROWS)
    for which in range(3):
        part(which).wait_recv()
        total = total + part_recv[which]
    ret_src[0] = total
    ret[0] = total
    for k in range(SLOTS - 1, 0, -1):
        pltpu.make_async_remote_copy(
            src_ref=ret_src.at[0],
            dst_ref=ret.at[k],
            send_sem=ret_ssem,
            recv_sem=ret_rsem,
            device_id=plane(-NEAREST[k % RING], -NEAREST[k // RING]),
            device_id_type=MESH,
        ).start()

    for sent, sem in ((send_buf, one_send), (middle, two_send)):
        most = sent.at[pl.ds(1, RING - 1)]
        pltpu.make_async_copy(most, most, sem).wait()
    for g in range(GROUPS):
        for which in (1, 2, 3):
            forward(which, g).wait_send()
    for which in range(3):
        part(which).wait_send()
    back = ret.at[pl.ds(1, SLOTS - 1)]
    pltpu.make_async_copy(back, back, ret_rsem).wait()

    lane = lax.broadcasted_iota(jnp.int32, (SLOTS, 1, LANES), 2)
    at = lax.broadcasted_iota(jnp.int32, (SLOTS, 1, LANES), 0)
    mine = jnp.sum(jnp.where(lax.div(lane, 2) == at, ret[...], 0.0), axis=0)
    column = jnp.sum(jnp.where(eye(ROWS), mine, 0.0), axis=1, keepdims=True)
    out_ref[...] = jnp.sum(jnp.where(chosen, column, 0.0), axis=0, keepdims=True)
    pltpu.make_async_copy(back, back, ret_ssem).wait()


def shards(embeddings, cluster_ids):
    docs, width = embeddings.shape
    vmem = pl.BlockSpec(memory_space=pltpu.VMEM)
    bf16, f32 = jnp.bfloat16, jnp.float32
    out = pl.pallas_call(
        functools.partial(kernel, math.sqrt(width)),
        out_shape=jax.ShapeDtypeStruct((1, docs), f32),
        in_specs=[pl.BlockSpec(memory_space=pl.ANY)] * 2,
        out_specs=vmem,
        scratch_shapes=[
            pltpu.VMEM((RING, RING, 16, LANES), bf16),
            pltpu.VMEM((RING, RING, 16, LANES), bf16),
            pltpu.VMEM((4, SLOTS, 16, LANES), bf16),
            pltpu.VMEM((4 * ROWS, width), bf16),
            pltpu.VMEM((3, 1, LANES), f32),
            pltpu.VMEM((3, 1, LANES), f32),
            pltpu.VMEM((1, 1, LANES), f32),
            pltpu.VMEM((SLOTS, 1, LANES), f32),
            pltpu.SemaphoreType.DMA,
            pltpu.SemaphoreType.DMA((RING,)),
            pltpu.SemaphoreType.DMA,
            pltpu.SemaphoreType.DMA((RING, len(PIECES))),
            pltpu.SemaphoreType.DMA((3, GROUPS)),
            pltpu.SemaphoreType.DMA((3, GROUPS)),
            pltpu.SemaphoreType.DMA((3,)),
            pltpu.SemaphoreType.DMA((3,)),
            pltpu.SemaphoreType.DMA,
            pltpu.SemaphoreType.DMA,
            pltpu.VMEM((docs, width), bf16),
            pltpu.VMEM((1, docs), jnp.int32),
            pltpu.SemaphoreType.DMA((2,)),
        ],
        compiler_params=pltpu.CompilerParams(collective_id=0, has_side_effects=True),
    )(embeddings, cluster_ids.reshape(1, docs))
    return out.reshape(docs) * (1.0 / (docs * Y))


def solution(mesh):
    placed = (P(("dp", "group"), None), P(("dp", "group"), None))
    return jax.shard_map(
        shards, mesh=mesh, in_specs=placed, out_specs=P(("dp", "group")), check_vma=False
    )
```

```python
import functools
import math

import jax
import jax.numpy as jnp
from jax import lax
from jax.experimental import pallas as pl
from jax.experimental.pallas import tpu as pltpu
from jax.sharding import PartitionSpec as P

MESH = pl.DeviceIdType.MESH
epsilon = 1e-06
Z, X, Y, CORES = 8, 4, 8, 2
SLOTS = Z * Y
PER = 2
ROWS = SLOTS * PER
CHUNKS = 8
LANES = 128

RING = 8
NEAREST = [0, 1, 7, 2, 6, 3, 5, 4]
PIECES = [(0, 1), (1, 8)]
GROUPS = SLOTS // RING
FIRST_ORDER = [7, 6, 5, 4, 3, 2, 1]
SECOND_ORDER = [1, 2, 3, 4, 5, 6, 7]


def offset_of(place):
    half = lax.div(place + 1, 2)
    return jnp.where(lax.rem(place, 2) == 1, half, lax.rem(RING - half, RING))


def wrap(value, size):
    return lax.rem(value + size, size)


def eye(size):
    return lax.broadcasted_iota(jnp.int32, (size, size), 0) == lax.broadcasted_iota(
        jnp.int32, (size, size), 1
    )


def permutation(tile_major):
    out = lax.broadcasted_iota(jnp.int32, (ROWS, ROWS), 0)
    src = lax.broadcasted_iota(jnp.int32, (ROWS, ROWS), 1)
    wanted = (lax.rem(lax.div(out, 2), 8) * 8 + lax.div(out, 16)) * 2 + lax.rem(out, 2)
    return (src == wanted).astype(jnp.float32).astype(jnp.bfloat16)


def dot_t(left, right):
    return lax.dot_general(
        left, right, (((1,), (1,)), ((), ())), preferred_element_type=jnp.float32
    )


def kernel(
    sharpen,
    x_hbm,
    ids_hbm,
    out_ref,
    send_buf,
    middle,
    raw,
    blocks,
    part_send,
    part_recv,
    ret_src,
    ret,
    one_send,
    one_recv,
    two_send,
    two_recv,
    fwd_send,
    fwd_recv,
    part_ssem,
    part_rsem,
    ret_ssem,
    ret_rsem,
    x_ref,
    ids_ref,
    in_sem,
):
    dp, y = lax.axis_index("dp"), lax.axis_index("group")
    z = lax.div(dp, X * CORES)
    x = lax.rem(lax.div(dp, CORES), X)
    core = lax.rem(dp, CORES)
    other = 1 - core
    right, left = wrap(x + 1, X), wrap(x - 1, X)

    def device(zz, xx, cc, yy):
        return ((zz * X + xx) * CORES + cc, yy)

    def plane(first, second):
        dz = second + core * (first - second)
        dy = first + core * (second - first)
        return device(wrap(z + dz, Z), x, core, wrap(y + dy, Y))

    partner = device(z, x, other, y)
    swap = lax.div(right, 2)
    own_swap = lax.div(x, 2)
    to_right = device(z, right, core + swap * (1 - 2 * core), y)
    to_left = device(z, left, core, y)
    from_right = device(z, right, core, y)
    from_left = device(z, left, core + own_swap * (1 - 2 * core), y)

    load_x = pltpu.make_async_copy(x_hbm, x_ref, in_sem.at[0])
    load_ids = pltpu.make_async_copy(ids_hbm, ids_ref, in_sem.at[1])
    load_x.start()
    load_ids.start()
    barrier = pltpu.get_barrier_semaphore()
    for away in NEAREST[:0:-1]:
        for target in (plane(away, 0), plane(0, away)):
            pl.semaphore_signal(barrier, inc=1, device_id=target, device_id_type=MESH)
    near = [partner] + [device(z, xx, cc, y) for xx in (left, right) for cc in (0, 1)]
    for target in near:
        pl.semaphore_signal(barrier, inc=1, device_id=target, device_id_type=MESH)

    load_x.wait()
    load_ids.wait()

    docs = x_ref.shape[0]
    widened = x_ref[...].astype(jnp.float32)
    normed = (
        widened / jnp.sqrt(jnp.sum(widened * widened, axis=1, keepdims=True) + epsilon)
    ).astype(jnp.bfloat16)

    ids_row = ids_ref[...]
    ids_col = jnp.sum(jnp.where(eye(docs), ids_row, 0), axis=1, keepdims=True)
    earlier = lax.broadcasted_iota(jnp.int32, (docs, docs), 0) < lax.broadcasted_iota(
        jnp.int32, (docs, docs), 1
    )
    within = jnp.sum(jnp.where((ids_col == ids_row) & earlier, 1, 0), axis=0, keepdims=True)
    slot_row = lax.broadcasted_iota(jnp.int32, (ROWS, 1), 0)
    slot = lax.div(slot_row, 2)
    first, second = offset_of(lax.rem(slot, RING)), offset_of(lax.div(slot, RING))
    owner_z = lax.rem(z + second + core * (first - second), Z)
    owner_y = lax.rem(y + first + core * (second - first), Y)
    owner = owner_z * Y + owner_y
    chosen = (owner == ids_row) & (lax.rem(slot_row, 2) == within)
    onehot = jnp.where(chosen, 1.0, 0.0)
    empty = jnp.sum(onehot, axis=1, keepdims=True) == 0.0

    packed = jnp.dot(onehot.astype(jnp.bfloat16), normed, preferred_element_type=jnp.float32)
    first = lax.broadcasted_iota(jnp.int32, packed.shape, 1) == 0
    packed = jnp.where(empty & first, 2.0, packed).astype(jnp.bfloat16)
    perm = permutation(True)
    stacked = jnp.concatenate(
        [
            jnp.concatenate(
                [packed[16 * g : 16 * g + 16, LANES * k : LANES * k + LANES] for k in range(CHUNKS)],
                axis=0,
            )
            for g in range(GROUPS)
        ],
        axis=1,
    )
    tiles = jnp.dot(perm, stacked, preferred_element_type=jnp.float32).astype(jnp.bfloat16)
    for k in range(SLOTS):
        g, row = k // 8, 16 * (k % 8)
        tile = tiles[row : row + 16, LANES * g : LANES * g + LANES]
        if k % RING == 0:
            middle[g, 0] = tile
        else:
            send_buf[k % RING, g] = tile

    pl.semaphore_wait(barrier, 2 * (RING - 1) + len(near))

    def along_first(a):
        return pltpu.make_async_remote_copy(
            src_ref=send_buf.at[a],
            dst_ref=middle.at[pl.ds(0, RING), a],
            send_sem=one_send,
            recv_sem=one_recv.at[a],
            device_id=plane(NEAREST[a], 0),
            device_id_type=MESH,
        )

    def along_second(b, piece):
        low, high = PIECES[piece]
        return pltpu.make_async_remote_copy(
            src_ref=middle.at[b, pl.ds(low, high - low)],
            dst_ref=raw.at[0, pl.ds(b * RING + low, high - low)],
            send_sem=two_send,
            recv_sem=two_recv.at[b, piece],
            device_id=plane(0, NEAREST[b]),
            device_id_type=MESH,
        )

    for a in FIRST_ORDER:
        along_first(a).start()
    for piece, (low, high) in enumerate(PIECES):
        for a in range(max(low, 1), high):
            along_first(a).wait_recv()
        for b in SECOND_ORDER:
            along_second(b, piece).start()

    def convert(which, row, g):
        got = middle[0] if which == 0 and g == 0 else raw[which, 8 * g : 8 * g + 8]
        got = got.reshape(ROWS, LANES)
        turned = jnp.dot(perm, got, preferred_element_type=jnp.float32).astype(jnp.bfloat16)
        for k in range(CHUNKS):
            blocks[row + 16 * g : row + 16 * g + 16, LANES * k : LANES * k + LANES] = turned[
                16 * k : 16 * k + 16
            ]

    starts = (ROWS, 2 * ROWS, 0, 3 * ROWS)
    targets = (None, partner, to_left, to_right)

    def forward(which, g):
        return pltpu.make_async_remote_copy(
            src_ref=middle.at[0] if g == 0 else raw.at[0, pl.ds(8 * g, 8)],
            dst_ref=raw.at[which, pl.ds(8 * g, 8)],
            send_sem=fwd_send.at[which - 1, g],
            recv_sem=fwd_recv.at[which - 1, g],
            device_id=targets[which],
            device_id_type=MESH,
        )

    for g in range(GROUPS):
        if g > 0:
            for piece in range(len(PIECES)):
                along_second(g, piece).wait_recv()
        for which in (3, 2, 1):
            forward(which, g).start()
        convert(0, starts[0], g)
    for g in range(GROUPS):
        for which in (1, 2, 3):
            forward(which, g).wait_recv()
            convert(which, starts[which], g)

    from_r, own, mate, from_l = (pl.ds(start, ROWS) for start in (0, ROWS, 2 * ROWS, 3 * ROWS))

    def column_sums(rows, columns, diagonal_at=None):
        source = blocks[rows, :]
        scores = dot_t(source, blocks[columns, :])
        keep = source[:, 0:1].astype(jnp.float32) < 1.5
        if diagonal_at is not None:
            keep = keep & (
                lax.broadcasted_iota(jnp.int32, scores.shape, 0)
                != lax.broadcasted_iota(jnp.int32, scores.shape, 1) + diagonal_at
            )
        return jnp.sum(
            jnp.where(keep, jnp.exp(scores * sharpen), 0.0), axis=0, keepdims=True
        )

    part_send[0] = column_sums(pl.ds(ROWS, 3 * ROWS), from_r)
    both = column_sums(from_r, pl.ds(2 * ROWS, 2 * ROWS))
    part_send[1] = both[:, :ROWS]
    part_send[2] = both[:, ROWS:]

    def part(which):
        return pltpu.make_async_remote_copy(
            src_ref=part_send.at[which],
            dst_ref=part_recv.at[which],
            send_sem=part_ssem.at[which],
            recv_sem=part_rsem.at[which],
            device_id=(from_right, partner, from_left)[which],
            device_id_type=MESH,
        )

    for which in range(3):
        part(which).start()
    total = column_sums(pl.ds(0, 3 * ROWS), own, diagonal_at=ROWS)
    for which in range(3):
        part(which).wait_recv()
        total = total + part_recv[which]
    ret_src[0] = total
    ret[0] = total
    for k in range(SLOTS - 1, 0, -1):
        pltpu.make_async_remote_copy(
            src_ref=ret_src.at[0],
            dst_ref=ret.at[k],
            send_sem=ret_ssem,
            recv_sem=ret_rsem,
            device_id=plane(-NEAREST[k % RING], -NEAREST[k // RING]),
            device_id_type=MESH,
        ).start()

    for sent, sem in ((send_buf, one_send), (middle, two_send)):
        most = sent.at[pl.ds(1, RING - 1)]
        pltpu.make_async_copy(most, most, sem).wait()
    for g in range(GROUPS):
        for which in (1, 2, 3):
            forward(which, g).wait_send()
    for which in range(3):
        part(which).wait_send()
    back = ret.at[pl.ds(1, SLOTS - 1)]
    pltpu.make_async_copy(back, back, ret_rsem).wait()

    lane = lax.broadcasted_iota(jnp.int32, (SLOTS, 1, LANES), 2)
    at = lax.broadcasted_iota(jnp.int32, (SLOTS, 1, LANES), 0)
    mine = jnp.sum(jnp.where(lax.div(lane, 2) == at, ret[...], 0.0), axis=0)
    column = jnp.sum(jnp.where(eye(ROWS), mine, 0.0), axis=1, keepdims=True)
    out_ref[...] = jnp.sum(jnp.where(chosen, column, 0.0), axis=0, keepdims=True)
    pltpu.make_async_copy(back, back, ret_ssem).wait()


def shards(embeddings, cluster_ids):
    docs, width = embeddings.shape
    vmem = pl.BlockSpec(memory_space=pltpu.VMEM)
    bf16, f32 = jnp.bfloat16, jnp.float32
    out = pl.pallas_call(
        functools.partial(kernel, math.sqrt(width)),
        out_shape=pltpu.VMEM((1, docs), f32),
        in_specs=[pl.BlockSpec(memory_space=pl.ANY)] * 2,
        out_specs=vmem,
        scratch_shapes=[
            pltpu.VMEM((RING, RING, 16, LANES), bf16),
            pltpu.VMEM((RING, RING, 16, LANES), bf16),
            pltpu.VMEM((4, SLOTS, 16, LANES), bf16),
            pltpu.VMEM((4 * ROWS, width), bf16),
            pltpu.VMEM((3, 1, LANES), f32),
            pltpu.VMEM((3, 1, LANES), f32),
            pltpu.VMEM((1, 1, LANES), f32),
            pltpu.VMEM((SLOTS, 1, LANES), f32),
            pltpu.SemaphoreType.DMA,
            pltpu.SemaphoreType.DMA((RING,)),
            pltpu.SemaphoreType.DMA,
            pltpu.SemaphoreType.DMA((RING, len(PIECES))),
            pltpu.SemaphoreType.DMA((3, GROUPS)),
            pltpu.SemaphoreType.DMA((3, GROUPS)),
            pltpu.SemaphoreType.DMA((3,)),
            pltpu.SemaphoreType.DMA((3,)),
            pltpu.SemaphoreType.DMA,
            pltpu.SemaphoreType.DMA,
            pltpu.VMEM((docs, width), bf16),
            pltpu.VMEM((1, docs), jnp.int32),
            pltpu.SemaphoreType.DMA((2,)),
        ],
        compiler_params=pltpu.CompilerParams(collective_id=0, has_side_effects=True),
    )(embeddings, cluster_ids.reshape(1, docs))
    return out.reshape(docs) * (1.0 / (docs * Y))


def solution(mesh):
    placed = (P(("dp", "group"), None), P(("dp", "group"), None))
    return jax.shard_map(
        shards, mesh=mesh, in_specs=placed, out_specs=P(("dp", "group")), check_vma=False
    )
```

```python
import functools
import math

import jax
import jax.numpy as jnp
from jax import lax
from jax.experimental import pallas as pl
from jax.experimental.pallas import tpu as pltpu
from jax.sharding import PartitionSpec as P

MESH = pl.DeviceIdType.MESH
epsilon = 1e-06
Z, X, Y, CORES = 8, 4, 8, 2
SLOTS = Z * Y
PER = 2
ROWS = SLOTS * PER
CHUNKS = 8
LANES = 128

RING = 8
NEAREST = [0, 1, 7, 2, 6, 3, 5, 4]
PIECES = [(0, 1), (1, 8)]
GROUPS = SLOTS // RING
FIRST_ORDER = [7, 6, 5, 4, 3, 2, 1]
SECOND_ORDER = [1, 2, 3, 4, 5, 6, 7]


def offset_of(place):
    half = lax.div(place + 1, 2)
    return jnp.where(lax.rem(place, 2) == 1, half, lax.rem(RING - half, RING))


def wrap(value, size):
    return lax.rem(value + size, size)


def eye(size):
    return lax.broadcasted_iota(jnp.int32, (size, size), 0) == lax.broadcasted_iota(
        jnp.int32, (size, size), 1
    )


def permutation(tile_major):
    out = lax.broadcasted_iota(jnp.int32, (ROWS, ROWS), 0)
    src = lax.broadcasted_iota(jnp.int32, (ROWS, ROWS), 1)
    wanted = (lax.rem(lax.div(out, 2), 8) * 8 + lax.div(out, 16)) * 2 + lax.rem(out, 2)
    return (src == wanted).astype(jnp.float32).astype(jnp.bfloat16)


def dot_t(left, right):
    return lax.dot_general(
        left, right, (((1,), (1,)), ((), ())), preferred_element_type=jnp.float32
    )


def kernel(
    sharpen,
    x_hbm,
    ids_hbm,
    out_ref,
    send_buf,
    middle,
    raw,
    blocks,
    part_send,
    part_recv,
    ret_src,
    ret,
    one_send,
    one_recv,
    two_send,
    two_recv,
    fwd_send,
    fwd_recv,
    part_ssem,
    part_rsem,
    ret_ssem,
    ret_rsem,
    x_ref,
    ids_ref,
    in_sem,
):
    dp, y = lax.axis_index("dp"), lax.axis_index("group")
    z = lax.div(dp, X * CORES)
    x = lax.rem(lax.div(dp, CORES), X)
    core = lax.rem(dp, CORES)
    other = 1 - core
    right, left = wrap(x + 1, X), wrap(x - 1, X)

    def device(zz, xx, cc, yy):
        return ((zz * X + xx) * CORES + cc, yy)

    def plane(first, second):
        dz = second + core * (first - second)
        dy = first + core * (second - first)
        return device(wrap(z + dz, Z), x, core, wrap(y + dy, Y))

    partner = device(z, x, other, y)
    swap = lax.div(right, 2)
    own_swap = lax.div(x, 2)
    to_right = device(z, right, core + swap * (1 - 2 * core), y)
    to_left = device(z, left, core, y)
    from_right = device(z, right, core, y)
    from_left = device(z, left, core + own_swap * (1 - 2 * core), y)

    load_x = pltpu.make_async_copy(x_hbm, x_ref, in_sem.at[0])
    load_ids = pltpu.make_async_copy(ids_hbm, ids_ref, in_sem.at[1])
    load_x.start()
    load_ids.start()
    barrier = pltpu.get_barrier_semaphore()
    for away in NEAREST[:0:-1]:
        for target in (plane(away, 0), plane(0, away)):
            pl.semaphore_signal(barrier, inc=1, device_id=target, device_id_type=MESH)
    near = [partner] + [device(z, xx, cc, y) for xx in (left, right) for cc in (0, 1)]
    for target in near:
        pl.semaphore_signal(barrier, inc=1, device_id=target, device_id_type=MESH)

    load_x.wait()
    load_ids.wait()

    docs = x_ref.shape[0]
    widened = x_ref[...].astype(jnp.float32)
    normed = (
        widened / jnp.sqrt(jnp.sum(widened * widened, axis=1, keepdims=True) + epsilon)
    ).astype(jnp.bfloat16)

    ids_row = ids_ref[...]
    ids_col = jnp.sum(jnp.where(eye(docs), ids_row, 0), axis=1, keepdims=True)
    earlier = lax.broadcasted_iota(jnp.int32, (docs, docs), 0) < lax.broadcasted_iota(
        jnp.int32, (docs, docs), 1
    )
    within = jnp.sum(jnp.where((ids_col == ids_row) & earlier, 1, 0), axis=0, keepdims=True)
    slot_row = lax.broadcasted_iota(jnp.int32, (ROWS, 1), 0)
    slot = lax.div(slot_row, 2)
    first, second = offset_of(lax.rem(slot, RING)), offset_of(lax.div(slot, RING))
    owner_z = lax.rem(z + second + core * (first - second), Z)
    owner_y = lax.rem(y + first + core * (second - first), Y)
    owner = owner_z * Y + owner_y
    chosen = (owner == ids_row) & (lax.rem(slot_row, 2) == within)
    onehot = jnp.where(chosen, 1.0, 0.0)
    empty = jnp.sum(onehot, axis=1, keepdims=True) == 0.0

    packed = jnp.dot(onehot.astype(jnp.bfloat16), normed, preferred_element_type=jnp.float32)
    first = lax.broadcasted_iota(jnp.int32, packed.shape, 1) == 0
    packed = jnp.where(empty & first, 2.0, packed).astype(jnp.bfloat16)
    perm = permutation(True)
    stacked = jnp.concatenate(
        [
            jnp.concatenate(
                [packed[16 * g : 16 * g + 16, LANES * k : LANES * k + LANES] for k in range(CHUNKS)],
                axis=0,
            )
            for g in range(GROUPS)
        ],
        axis=1,
    )
    tiles = jnp.dot(perm, stacked, preferred_element_type=jnp.float32).astype(jnp.bfloat16)
    for k in range(SLOTS):
        g, row = k // 8, 16 * (k % 8)
        tile = tiles[row : row + 16, LANES * g : LANES * g + LANES]
        if k % RING == 0:
            middle[g, 0] = tile
        else:
            send_buf[k % RING, g] = tile

    pl.semaphore_wait(barrier, 2 * (RING - 1) + len(near))

    def along_first(a):
        return pltpu.make_async_remote_copy(
            src_ref=send_buf.at[a],
            dst_ref=middle.at[pl.ds(0, RING), a],
            send_sem=one_send,
            recv_sem=one_recv.at[a],
            device_id=plane(NEAREST[a], 0),
            device_id_type=MESH,
        )

    def along_second(b, piece):
        low, high = PIECES[piece]
        return pltpu.make_async_remote_copy(
            src_ref=middle.at[b, pl.ds(low, high - low)],
            dst_ref=raw.at[0, pl.ds(b * RING + low, high - low)],
            send_sem=two_send,
            recv_sem=two_recv.at[b, piece],
            device_id=plane(0, NEAREST[b]),
            device_id_type=MESH,
        )

    for a in FIRST_ORDER:
        along_first(a).start()
    for piece, (low, high) in enumerate(PIECES):
        for a in range(max(low, 1), high):
            along_first(a).wait_recv()
        for b in SECOND_ORDER:
            along_second(b, piece).start()

    def convert(which, row, g):
        got = middle[0] if which == 0 and g == 0 else raw[which, 8 * g : 8 * g + 8]
        got = got.reshape(ROWS, LANES)
        turned = jnp.dot(perm, got, preferred_element_type=jnp.float32).astype(jnp.bfloat16)
        for k in range(CHUNKS):
            blocks[row + 16 * g : row + 16 * g + 16, LANES * k : LANES * k + LANES] = turned[
                16 * k : 16 * k + 16
            ]

    starts = (ROWS, 2 * ROWS, 0, 3 * ROWS)
    targets = (None, partner, to_left, to_right)

    UNITS = [(0, 1), (1, 3), (3, 5), (5, 7), (7, 8)]

    def forward(which, unit):
        low, high = UNITS[unit]
        at = pl.ds(low * RING, (high - low) * RING)
        return pltpu.make_async_remote_copy(
            src_ref=middle.at[0] if unit == 0 else raw.at[0, at],
            dst_ref=raw.at[which, at],
            send_sem=fwd_send.at[which - 1, unit],
            recv_sem=fwd_recv.at[which - 1, unit],
            device_id=targets[which],
            device_id_type=MESH,
        )

    for unit, (low, high) in enumerate(UNITS):
        for b in range(low, high):
            if b > 0:
                for piece in range(len(PIECES)):
                    along_second(b, piece).wait_recv()
        for which in (3, 2, 1):
            forward(which, unit).start()
        for b in range(low, high):
            convert(0, starts[0], b)
    for unit, (low, high) in enumerate(UNITS):
        for which in (1, 2, 3):
            forward(which, unit).wait_recv()
            for b in range(low, high):
                convert(which, starts[which], b)

    from_r, own, mate, from_l = (pl.ds(start, ROWS) for start in (0, ROWS, 2 * ROWS, 3 * ROWS))

    def column_sums(rows, columns, diagonal_at=None):
        source = blocks[rows, :]
        scores = dot_t(source, blocks[columns, :])
        keep = source[:, 0:1].astype(jnp.float32) < 1.5
        if diagonal_at is not None:
            keep = keep & (
                lax.broadcasted_iota(jnp.int32, scores.shape, 0)
                != lax.broadcasted_iota(jnp.int32, scores.shape, 1) + diagonal_at
            )
        return jnp.sum(
            jnp.where(keep, jnp.exp(scores * sharpen), 0.0), axis=0, keepdims=True
        )

    part_send[0] = column_sums(pl.ds(ROWS, 3 * ROWS), from_r)
    both = column_sums(from_r, pl.ds(2 * ROWS, 2 * ROWS))
    part_send[1] = both[:, :ROWS]
    part_send[2] = both[:, ROWS:]

    def part(which):
        return pltpu.make_async_remote_copy(
            src_ref=part_send.at[which],
            dst_ref=part_recv.at[which],
            send_sem=part_ssem.at[which],
            recv_sem=part_rsem.at[which],
            device_id=(from_right, partner, from_left)[which],
            device_id_type=MESH,
        )

    for which in range(3):
        part(which).start()
    total = column_sums(pl.ds(0, 3 * ROWS), own, diagonal_at=ROWS)
    for which in range(3):
        part(which).wait_recv()
        total = total + part_recv[which]
    ret_src[0] = total
    ret[0] = total
    for k in range(SLOTS - 1, 0, -1):
        pltpu.make_async_remote_copy(
            src_ref=ret_src.at[0],
            dst_ref=ret.at[k],
            send_sem=ret_ssem,
            recv_sem=ret_rsem,
            device_id=plane(-NEAREST[k % RING], -NEAREST[k // RING]),
            device_id_type=MESH,
        ).start()

    for sent, sem in ((send_buf, one_send), (middle, two_send)):
        most = sent.at[pl.ds(1, RING - 1)]
        pltpu.make_async_copy(most, most, sem).wait()
    for unit in range(len(UNITS)):
        for which in (1, 2, 3):
            forward(which, unit).wait_send()
    for which in range(3):
        part(which).wait_send()
    back = ret.at[pl.ds(1, SLOTS - 1)]
    pltpu.make_async_copy(back, back, ret_rsem).wait()

    lane = lax.broadcasted_iota(jnp.int32, (SLOTS, 1, LANES), 2)
    at = lax.broadcasted_iota(jnp.int32, (SLOTS, 1, LANES), 0)
    mine = jnp.sum(jnp.where(lax.div(lane, 2) == at, ret[...], 0.0), axis=0)
    column = jnp.sum(jnp.where(eye(ROWS), mine, 0.0), axis=1, keepdims=True)
    out_ref[...] = jnp.sum(jnp.where(chosen, column, 0.0), axis=0, keepdims=True)
    pltpu.make_async_copy(back, back, ret_ssem).wait()


def shards(embeddings, cluster_ids):
    docs, width = embeddings.shape
    vmem = pl.BlockSpec(memory_space=pltpu.VMEM)
    bf16, f32 = jnp.bfloat16, jnp.float32
    out = pl.pallas_call(
        functools.partial(kernel, math.sqrt(width)),
        out_shape=pltpu.VMEM((1, docs), f32),
        in_specs=[pl.BlockSpec(memory_space=pl.ANY)] * 2,
        out_specs=vmem,
        scratch_shapes=[
            pltpu.VMEM((RING, RING, 16, LANES), bf16),
            pltpu.VMEM((RING, RING, 16, LANES), bf16),
            pltpu.VMEM((4, SLOTS, 16, LANES), bf16),
            pltpu.VMEM((4 * ROWS, width), bf16),
            pltpu.VMEM((3, 1, LANES), f32),
            pltpu.VMEM((3, 1, LANES), f32),
            pltpu.VMEM((1, 1, LANES), f32),
            pltpu.VMEM((SLOTS, 1, LANES), f32),
            pltpu.SemaphoreType.DMA,
            pltpu.SemaphoreType.DMA((RING,)),
            pltpu.SemaphoreType.DMA,
            pltpu.SemaphoreType.DMA((RING, len(PIECES))),
            pltpu.SemaphoreType.DMA((3, GROUPS)),
            pltpu.SemaphoreType.DMA((3, GROUPS)),
            pltpu.SemaphoreType.DMA((3,)),
            pltpu.SemaphoreType.DMA((3,)),
            pltpu.SemaphoreType.DMA,
            pltpu.SemaphoreType.DMA,
            pltpu.VMEM((docs, width), bf16),
            pltpu.VMEM((1, docs), jnp.int32),
            pltpu.SemaphoreType.DMA((2,)),
        ],
        compiler_params=pltpu.CompilerParams(collective_id=0, has_side_effects=True),
    )(embeddings, cluster_ids.reshape(1, docs))
    return out.reshape(docs) * (1.0 / (docs * Y))


def solution(mesh):
    placed = (P(("dp", "group"), None), P(("dp", "group"), None))
    return jax.shard_map(
        shards, mesh=mesh, in_specs=placed, out_specs=P(("dp", "group")), check_vma=False
    )
```

```python
import functools
import math

import jax
import jax.numpy as jnp
from jax import lax
from jax.experimental import pallas as pl
from jax.experimental.pallas import tpu as pltpu
from jax.sharding import PartitionSpec as P

MESH = pl.DeviceIdType.MESH
epsilon = 1e-06
Z, X, Y, CORES = 8, 4, 8, 2
SLOTS = Z * Y
PER = 2
ROWS = SLOTS * PER
CHUNKS = 8
LANES = 128

RING = 8
NEAREST = [0, 1, 7, 2, 6, 3, 5, 4]
PIECES = [(0, 1), (1, 8)]
GROUPS = SLOTS // RING
FIRST_ORDER = [7, 6, 5, 4, 3, 2, 1]
SECOND_ORDER = [1, 2, 3, 4, 5, 6, 7]


def offset_of(place):
    half = lax.div(place + 1, 2)
    return jnp.where(lax.rem(place, 2) == 1, half, lax.rem(RING - half, RING))


def wrap(value, size):
    return lax.rem(value + size, size)


def eye(size):
    return lax.broadcasted_iota(jnp.int32, (size, size), 0) == lax.broadcasted_iota(
        jnp.int32, (size, size), 1
    )


def permutation(tile_major):
    out = lax.broadcasted_iota(jnp.int32, (ROWS, ROWS), 0)
    src = lax.broadcasted_iota(jnp.int32, (ROWS, ROWS), 1)
    wanted = (lax.rem(lax.div(out, 2), 8) * 8 + lax.div(out, 16)) * 2 + lax.rem(out, 2)
    return (src == wanted).astype(jnp.float32).astype(jnp.bfloat16)


def dot_t(left, right):
    return lax.dot_general(
        left, right, (((1,), (1,)), ((), ())), preferred_element_type=jnp.float32
    )


def kernel(
    sharpen,
    x_hbm,
    ids_hbm,
    out_ref,
    send_buf,
    middle,
    raw,
    blocks,
    part_send,
    part_recv,
    ret_src,
    ret,
    one_send,
    one_recv,
    two_send,
    two_recv,
    fwd_send,
    fwd_recv,
    part_ssem,
    part_rsem,
    ret_ssem,
    ret_rsem,
    x_ref,
    ids_ref,
    in_sem,
):
    dp, y = lax.axis_index("dp"), lax.axis_index("group")
    z = lax.div(dp, X * CORES)
    x = lax.rem(lax.div(dp, CORES), X)
    core = lax.rem(dp, CORES)
    other = 1 - core
    right, left = wrap(x + 1, X), wrap(x - 1, X)

    def device(zz, xx, cc, yy):
        return ((zz * X + xx) * CORES + cc, yy)

    def plane(first, second):
        dz = second + core * (first - second)
        dy = first + core * (second - first)
        return device(wrap(z + dz, Z), x, core, wrap(y + dy, Y))

    partner = device(z, x, other, y)
    swap = lax.div(right, 2)
    own_swap = lax.div(x, 2)
    to_right = device(z, right, core + swap * (1 - 2 * core), y)
    to_left = device(z, left, core, y)
    from_right = device(z, right, core, y)
    from_left = device(z, left, core + own_swap * (1 - 2 * core), y)

    load_x = pltpu.make_async_copy(x_hbm, x_ref, in_sem.at[0])
    load_ids = pltpu.make_async_copy(ids_hbm, ids_ref, in_sem.at[1])
    load_x.start()
    load_ids.start()
    barrier = pltpu.get_barrier_semaphore()
    for away in NEAREST[:0:-1]:
        for target in (plane(away, 0), plane(0, away)):
            pl.semaphore_signal(barrier, inc=1, device_id=target, device_id_type=MESH)
    near = [partner] + [device(z, xx, cc, y) for xx in (left, right) for cc in (0, 1)]
    for target in near:
        pl.semaphore_signal(barrier, inc=1, device_id=target, device_id_type=MESH)

    load_x.wait()
    load_ids.wait()

    docs = x_ref.shape[0]
    widened = x_ref[...].astype(jnp.float32)
    normed = (
        widened / jnp.sqrt(jnp.sum(widened * widened, axis=1, keepdims=True) + epsilon)
    ).astype(jnp.bfloat16)

    ids_row = ids_ref[...]
    ids_col = jnp.sum(jnp.where(eye(docs), ids_row, 0), axis=1, keepdims=True)
    earlier = lax.broadcasted_iota(jnp.int32, (docs, docs), 0) < lax.broadcasted_iota(
        jnp.int32, (docs, docs), 1
    )
    within = jnp.sum(jnp.where((ids_col == ids_row) & earlier, 1, 0), axis=0, keepdims=True)
    slot_row = lax.broadcasted_iota(jnp.int32, (ROWS, 1), 0)
    slot = lax.div(slot_row, 2)
    first, second = offset_of(lax.rem(slot, RING)), offset_of(lax.div(slot, RING))
    owner_z = lax.rem(z + second + core * (first - second), Z)
    owner_y = lax.rem(y + first + core * (second - first), Y)
    owner = owner_z * Y + owner_y
    chosen = (owner == ids_row) & (lax.rem(slot_row, 2) == within)
    onehot = jnp.where(chosen, 1.0, 0.0)
    empty = jnp.sum(onehot, axis=1, keepdims=True) == 0.0

    packed = jnp.dot(onehot.astype(jnp.bfloat16), normed, preferred_element_type=jnp.float32)
    first = lax.broadcasted_iota(jnp.int32, packed.shape, 1) == 0
    packed = jnp.where(empty & first, 2.0, packed).astype(jnp.bfloat16)
    perm = permutation(True)
    stacked = jnp.concatenate(
        [
            jnp.concatenate(
                [packed[16 * g : 16 * g + 16, LANES * k : LANES * k + LANES] for k in range(CHUNKS)],
                axis=0,
            )
            for g in range(GROUPS)
        ],
        axis=1,
    )
    tiles = jnp.dot(perm, stacked, preferred_element_type=jnp.float32).astype(jnp.bfloat16)
    for k in range(SLOTS):
        g, row = k // 8, 16 * (k % 8)
        tile = tiles[row : row + 16, LANES * g : LANES * g + LANES]
        if k % RING == 0:
            middle[g, 0] = tile
        else:
            send_buf[k % RING, g] = tile

    pl.semaphore_wait(barrier, 2 * (RING - 1) + len(near))

    def along_first(a):
        return pltpu.make_async_remote_copy(
            src_ref=send_buf.at[a],
            dst_ref=middle.at[pl.ds(0, RING), a],
            send_sem=one_send,
            recv_sem=one_recv.at[a],
            device_id=plane(NEAREST[a], 0),
            device_id_type=MESH,
        )

    def along_second(b, piece):
        low, high = PIECES[piece]
        return pltpu.make_async_remote_copy(
            src_ref=middle.at[b, pl.ds(low, high - low)],
            dst_ref=raw.at[0, pl.ds(b * RING + low, high - low)],
            send_sem=two_send,
            recv_sem=two_recv.at[b, piece],
            device_id=plane(0, NEAREST[b]),
            device_id_type=MESH,
        )

    for a in FIRST_ORDER:
        along_first(a).start()
    for piece, (low, high) in enumerate(PIECES):
        for a in range(max(low, 1), high):
            along_first(a).wait_recv()
        for b in SECOND_ORDER:
            along_second(b, piece).start()

    def convert(which, row, g):
        got = middle[0] if which == 0 and g == 0 else raw[which, 8 * g : 8 * g + 8]
        got = got.reshape(ROWS, LANES)
        turned = jnp.dot(perm, got, preferred_element_type=jnp.float32).astype(jnp.bfloat16)
        for k in range(CHUNKS):
            blocks[row + 16 * g : row + 16 * g + 16, LANES * k : LANES * k + LANES] = turned[
                16 * k : 16 * k + 16
            ]

    starts = (ROWS, 2 * ROWS, 0, 3 * ROWS)
    targets = (None, partner, to_left, to_right)

    UNITS = [(0, 1), (1, 3), (3, 5), (5, 7), (7, 8)]

    def forward(which, unit):
        low, high = UNITS[unit]
        at = pl.ds(low * RING, (high - low) * RING)
        return pltpu.make_async_remote_copy(
            src_ref=middle.at[0] if unit == 0 else raw.at[0, at],
            dst_ref=raw.at[which, at],
            send_sem=fwd_send.at[which - 1, unit],
            recv_sem=fwd_recv.at[which - 1, unit],
            device_id=targets[which],
            device_id_type=MESH,
        )

    for unit, (low, high) in enumerate(UNITS):
        for b in range(low, high):
            if b > 0:
                for piece in range(len(PIECES)):
                    along_second(b, piece).wait_recv()
        for which in (2, 3, 1):
            forward(which, unit).start()
        for b in range(low, high):
            convert(0, starts[0], b)
    for unit, (low, high) in enumerate(UNITS):
        for which in (1, 2, 3):
            forward(which, unit).wait_recv()
            for b in range(low, high):
                convert(which, starts[which], b)

    from_r, own, mate, from_l = (pl.ds(start, ROWS) for start in (0, ROWS, 2 * ROWS, 3 * ROWS))

    def column_sums(rows, columns, diagonal_at=None):
        source = blocks[rows, :]
        scores = dot_t(source, blocks[columns, :])
        keep = source[:, 0:1].astype(jnp.float32) < 1.5
        if diagonal_at is not None:
            keep = keep & (
                lax.broadcasted_iota(jnp.int32, scores.shape, 0)
                != lax.broadcasted_iota(jnp.int32, scores.shape, 1) + diagonal_at
            )
        return jnp.sum(
            jnp.where(keep, jnp.exp(scores * sharpen), 0.0), axis=0, keepdims=True
        )

    part_send[0] = column_sums(pl.ds(ROWS, 3 * ROWS), from_r)
    both = column_sums(from_r, pl.ds(2 * ROWS, 2 * ROWS))
    part_send[1] = both[:, :ROWS]
    part_send[2] = both[:, ROWS:]

    def part(which):
        return pltpu.make_async_remote_copy(
            src_ref=part_send.at[which],
            dst_ref=part_recv.at[which],
            send_sem=part_ssem.at[which],
            recv_sem=part_rsem.at[which],
            device_id=(from_right, partner, from_left)[which],
            device_id_type=MESH,
        )

    for which in range(3):
        part(which).start()
    total = column_sums(pl.ds(0, 3 * ROWS), own, diagonal_at=ROWS)
    for which in range(3):
        part(which).wait_recv()
        total = total + part_recv[which]
    ret_src[0] = total
    ret[0] = total
    for k in range(SLOTS - 1, 0, -1):
        pltpu.make_async_remote_copy(
            src_ref=ret_src.at[0],
            dst_ref=ret.at[k],
            send_sem=ret_ssem,
            recv_sem=ret_rsem,
            device_id=plane(-NEAREST[k % RING], -NEAREST[k // RING]),
            device_id_type=MESH,
        ).start()

    for sent, sem in ((send_buf, one_send), (middle, two_send)):
        most = sent.at[pl.ds(1, RING - 1)]
        pltpu.make_async_copy(most, most, sem).wait()
    for unit in range(len(UNITS)):
        for which in (1, 2, 3):
            forward(which, unit).wait_send()
    for which in range(3):
        part(which).wait_send()
    back = ret.at[pl.ds(1, SLOTS - 1)]
    pltpu.make_async_copy(back, back, ret_rsem).wait()

    lane = lax.broadcasted_iota(jnp.int32, (SLOTS, 1, LANES), 2)
    at = lax.broadcasted_iota(jnp.int32, (SLOTS, 1, LANES), 0)
    mine = jnp.sum(jnp.where(lax.div(lane, 2) == at, ret[...], 0.0), axis=0)
    column = jnp.sum(jnp.where(eye(ROWS), mine, 0.0), axis=1, keepdims=True)
    out_ref[...] = jnp.sum(jnp.where(chosen, column, 0.0), axis=0, keepdims=True)
    pltpu.make_async_copy(back, back, ret_ssem).wait()


def shards(embeddings, cluster_ids):
    docs, width = embeddings.shape
    vmem = pl.BlockSpec(memory_space=pltpu.VMEM)
    bf16, f32 = jnp.bfloat16, jnp.float32
    out = pl.pallas_call(
        functools.partial(kernel, math.sqrt(width)),
        out_shape=pltpu.VMEM((1, docs), f32),
        in_specs=[pl.BlockSpec(memory_space=pl.ANY)] * 2,
        out_specs=vmem,
        scratch_shapes=[
            pltpu.VMEM((RING, RING, 16, LANES), bf16),
            pltpu.VMEM((RING, RING, 16, LANES), bf16),
            pltpu.VMEM((4, SLOTS, 16, LANES), bf16),
            pltpu.VMEM((4 * ROWS, width), bf16),
            pltpu.VMEM((3, 1, LANES), f32),
            pltpu.VMEM((3, 1, LANES), f32),
            pltpu.VMEM((1, 1, LANES), f32),
            pltpu.VMEM((SLOTS, 1, LANES), f32),
            pltpu.SemaphoreType.DMA,
            pltpu.SemaphoreType.DMA((RING,)),
            pltpu.SemaphoreType.DMA,
            pltpu.SemaphoreType.DMA((RING, len(PIECES))),
            pltpu.SemaphoreType.DMA((3, GROUPS)),
            pltpu.SemaphoreType.DMA((3, GROUPS)),
            pltpu.SemaphoreType.DMA((3,)),
            pltpu.SemaphoreType.DMA((3,)),
            pltpu.SemaphoreType.DMA,
            pltpu.SemaphoreType.DMA,
            pltpu.VMEM((docs, width), bf16),
            pltpu.VMEM((1, docs), jnp.int32),
            pltpu.SemaphoreType.DMA((2,)),
        ],
        compiler_params=pltpu.CompilerParams(collective_id=0, has_side_effects=True),
    )(embeddings, cluster_ids.reshape(1, docs))
    return out.reshape(docs) * (1.0 / (docs * Y))


def solution(mesh):
    placed = (P(("dp", "group"), None), P(("dp", "group"), None))
    return jax.shard_map(
        shards, mesh=mesh, in_specs=placed, out_specs=P(("dp", "group")), check_vma=False
    )
```
